32 devices in a mesh: rows: 4 (over y, core), shard: 8 (over z, x).
Axes of the slice: x: 2, y: 2, z: 4, core: 2. Of those that a mesh axis runs over, the one named last changes fastest.
Arguments:
- hidden_in: bfloat16 [128, 14336], P('rows', 'shard'), may hold values from -6 to 6
- resid: bfloat16 [128, 3584], P('rows'), may hold values from -6 to 6
- down_one: bfloat16 [14336, 3584], P('shard'), may hold values from -0.046875 to 0.046875
- gain_one: float32 [3584], replicated, may hold values from 0.5 to 1.5
- enc_weight: bfloat16 [3584, 65536], P(None, ('rows', 'shard')), may hold values from -0.09375 to 0.09375
- enc_bias: float32 [65536], P(('rows', 'shard')), may hold values from -3 to 3
- dec_weight: bfloat16 [65536, 3584], P(('rows', 'shard')), may hold values from -0.046875 to 0.046875
- dec_bias: float32 [3584], replicated, may hold values from -3 to 3
- gain_pre: float32 [3584], replicated, may hold values from 0.5 to 1.5
- gate_two: bfloat16 [3584, 14336], P(None, 'shard'), may hold values from -0.09375 to 0.09375
- up_two: bfloat16 [3584, 14336], P(None, 'shard'), may hold values from -0.09375 to 0.09375
- down_two: bfloat16 [14336, 3584], P('shard'), may hold values from -0.046875 to 0.046875
- gain_post: float32 [3584], replicated, may hold values from 0.5 to 1.5
Outputs:
- latents: bfloat16 [128, 65536], P(None, ('rows', 'shard'))
- delta: float32 [128, 3584], P('rows', 'shard')
The draws below stay inside these ranges and needn't reach their ends.
All inputs are finite; a program needn't handle non-finite values.
Results may differ from the reference program's by a relative error of at most 0.0064.
Values may be sent and summed in bfloat16 or wider, within the bound.
No kernel may reach another device: no remote copies, remote signals or barrier semaphores. Data moves between devices by JAX's collectives and lax.ppermute only.
A program may use at most 128 MiB of HBM per device.

```python
import jax
import jax.numpy as jnp
from jax import lax

D = 3584
FF = 14336
LAT = 65536
TOKENS = 128


def raised(result, own_key, source, target, blocks, factor):
    owner, partner = [(jnp.arange(result.shape[dim]) // (result.shape[dim] // blocks)).reshape([-1 if axis == dim else 1 for axis in range(result.ndim)]) for dim in (source, target)]
    chosen = jax.random.permutation(own_key, blocks)[partner]
    strong = (owner == chosen) | (owner == (partner + blocks // 2) % blocks)
    return jnp.where(strong, factor * result, result)


def levels(own_key, extent, pieces, least, high):
    factor_of, own = 1.0, jax.random.fold_in(own_key, 6)
    for axis_at, parts in pieces:
        heights = jnp.exp(jax.random.uniform(jax.random.fold_in(own, axis_at), (parts,), jnp.float32, least / len(pieces), high / len(pieces)))
        factor_of = factor_of * jnp.repeat(heights, extent[axis_at] // parts).reshape([-1 if axis == axis_at else 1 for axis in range(len(extent))])
    return factor_of


def bell_draw(rng, extent, scale, limit, cuts=(), held_as=jnp.bfloat16):
    level = levels(rng, extent, cuts, -0.22, 0.18) if cuts else 1.0
    values = jax.random.normal(rng, extent, jnp.float32) * scale * level
    return jnp.minimum(jnp.maximum(values, -limit), limit).astype(held_as)


def gaussian_with(own_key, shape, width, limit, cuts, heavy, kind=jnp.bfloat16):
    drawn = width * jax.random.normal(own_key, shape, jnp.float32)
    if cuts:
        drawn = drawn * levels(own_key, shape, cuts, -0.22, 0.18)
    return jnp.clip(raised(drawn, jax.random.fold_in(own_key, 3), *heavy), -limit, limit).astype(kind)


def setup_inputs(seed: int = 0) -> dict:
    keys = jax.random.split(jax.random.key(seed), 14)
    hidden_in = bell_draw(keys[0], (TOKENS, FF), 1.0, 6.0, ((0, 4), (1, 8)))
    resid = bell_draw(keys[1], (TOKENS, D), 1.0, 6.0, ((0, 4),))
    down_one = bell_draw(keys[2], (FF, D), FF ** -0.5, 0.046875, ((0, 8),))
    gain_one = jnp.clip(jax.random.uniform(keys[3], (D,), jnp.float32, 0.5, 1.5), 0.5, 1.5)
    enc_weight = bell_draw(keys[4], (D, LAT), D ** -0.5, 0.09375, ((1, 32),))
    enc_bias = bell_draw(keys[5], (LAT,), 0.5, 3.0, ((0, 32),), jnp.float32)
    dec_weight = gaussian_with(keys[6], (LAT, D), LAT ** -0.5, 0.046875, ((0, 32),), (0, 1, 32, 2.75))
    dec_bias = bell_draw(keys[7], (D,), 0.5, 3.0, (), jnp.float32)
    gain_pre = jnp.clip(jax.random.uniform(keys[8], (D,), jnp.float32, 0.5, 1.5), 0.5, 1.5)
    gate_two = bell_draw(keys[9], (D, FF), D ** -0.5, 0.09375, ((1, 8),))
    up_two = bell_draw(keys[10], (D, FF), D ** -0.5, 0.09375, ((1, 8),))
    down_two = bell_draw(keys[11], (FF, D), FF ** -0.5, 0.046875, ((0, 8),))
    gain_post = jnp.clip(jax.random.uniform(keys[12], (D,), jnp.float32, 0.5, 1.5), 0.5, 1.5)
    return dict(hidden_in=hidden_in, resid=resid, down_one=down_one, gain_one=gain_one, enc_weight=enc_weight, enc_bias=enc_bias, dec_weight=dec_weight, dec_bias=dec_bias, gain_pre=gain_pre, gate_two=gate_two, up_two=up_two, down_two=down_two, gain_post=gain_post)


def rms_scale(values, gain):
    mean_sq = lax.optimization_barrier(jnp.mean(values * values, axis=1, keepdims=True))
    return values * jax.lax.rsqrt(mean_sq + 1e-06) * gain

def layer_two(stream, gain_pre, gate_two, up_two, down_two, gain_post):
    upcast = stream.astype(jnp.float32)
    normed = rms_scale(upcast, gain_pre).astype(jnp.bfloat16)
    gate_out = jnp.dot(normed, gate_two, preferred_element_type=jnp.float32)
    up_out = jnp.dot(normed, up_two, preferred_element_type=jnp.float32)
    act = (jax.nn.gelu(gate_out, approximate=True) * up_out).astype(jnp.bfloat16)
    second = jnp.dot(act, down_two, preferred_element_type=jnp.float32)
    return upcast + rms_scale(second, gain_post)

def reference(hidden_in, resid, down_one, gain_one, enc_weight, enc_bias, dec_weight, dec_bias, gain_pre, gate_two, up_two, down_two, gain_post):
    first = jnp.dot(hidden_in, down_one, preferred_element_type=jnp.float32)
    clean = (resid.astype(jnp.float32) + rms_scale(first, gain_one)).astype(jnp.bfloat16)
    centered = (clean.astype(jnp.float32) - dec_bias).astype(jnp.bfloat16)
    pre_act = jnp.dot(centered, enc_weight, preferred_element_type=jnp.float32) + enc_bias
    latents = jnp.maximum(pre_act, 0.0).astype(jnp.bfloat16)
    recon = (jnp.dot(latents, dec_weight, preferred_element_type=jnp.float32) + dec_bias).astype(jnp.bfloat16)
    out_clean = layer_two(clean, gain_pre, gate_two, up_two, down_two, gain_post)
    out_recon = layer_two(recon, gain_pre, gate_two, up_two, down_two, gain_post)
    return (latents, out_recon - out_clean)
```

```python
import jax
import jax.numpy as jnp
from jax import lax
from jax.sharding import PartitionSpec as P

AXES = ("rows", "shard")
BF = jnp.bfloat16
F32 = jnp.float32


def swap(value, mask):
    total = lax.axis_size("rows") * lax.axis_size("shard")
    return lax.ppermute(value, AXES, [(i, i ^ mask) for i in range(total)])


def take(value, start, size, dim):
    return lax.dynamic_slice_in_dim(value, start, size, dim)


def sum_pieces(value, position, count, unit, dim):
    size = value.shape[dim] // count
    sent = value.astype(BF)
    total = take(value, position * size, size, dim).astype(F32)
    got = [swap(take(sent, (position ^ k) * size, size, dim), k * unit) for k in range(1, count)]
    for piece in got:
        total = total + piece.astype(F32)
    return total


def join_pieces(piece, position, count, unit, dim):
    size = piece.shape[dim]
    shape = list(piece.shape)
    shape[dim] = size * count
    got = [swap(piece, k * unit) for k in range(1, count)]
    whole = jnp.zeros(shape, piece.dtype)
    for k, part in enumerate([piece] + got):
        whole = lax.dynamic_update_slice_in_dim(whole, part, (position ^ k) * size, dim)
    return whole


def on_device(
    hidden_in,
    resid,
    down_one,
    gain_one,
    enc_weight,
    enc_bias,
    dec_weight,
    dec_bias,
    gain_pre,
    gate_two,
    up_two,
    down_two,
    gain_post,
):
    n_rows = lax.axis_size("rows")
    n_shard = lax.axis_size("shard")
    row = lax.axis_index("rows")
    shard = lax.axis_index("shard")
    group, width = resid.shape
    half = width // 2
    core, lane = row % 2, row // 2
    n_lane = n_rows // 2
    near, far = shard % 2, shard // 2
    n_far = n_shard // 2
    tokens = group // n_far
    core_unit, lane_unit, near_unit, far_unit = n_shard, 2 * n_shard, 1, 2

    first_part = jnp.dot(hidden_in, down_one, preferred_element_type=F32)
    first = sum_pieces(first_part, far, n_far, far_unit, 0)
    first_bf = first.astype(BF)
    first = first_bf.astype(F32) + swap(first_bf, near_unit).astype(F32)
    mean_sq = jnp.mean(first * first, axis=1, keepdims=True)
    resid_piece = take(resid, far * tokens, tokens, 0).astype(F32)
    clean_piece = (resid_piece + first * lax.rsqrt(mean_sq + 1e-06) * gain_one).astype(BF)
    clean_half = join_pieces(take(clean_piece, near * half, half, 1), far, n_far, far_unit, 0)

    other_half = swap(clean_half, near_unit)
    lanes = [[None] * 2 for _ in range(n_lane)]
    lanes[0] = [clean_half, other_half]
    for k in range(1, n_lane):
        lanes[k] = [swap(clean_half, k * lane_unit), swap(clean_half, k * lane_unit + near_unit)]
    mine = jnp.zeros((n_lane, group, width), BF)
    for k in range(n_lane):
        for j in range(2):
            mine = lax.dynamic_update_slice(
                mine, lanes[k][j][None], (lane ^ k, 0, (near ^ j) * half)
            )
    clean = lax.dynamic_index_in_dim(mine, lane, 0, keepdims=False)
    theirs = swap(mine, core_unit)
    clean_all = jnp.where(
        core == 0, jnp.stack([mine, theirs], axis=1), jnp.stack([theirs, mine], axis=1)
    ).reshape(n_rows * group, width)

    centered = (clean_all.astype(F32) - dec_bias).astype(BF)
    pre_act = jnp.dot(centered, enc_weight, preferred_element_type=F32) + enc_bias
    latents = jnp.maximum(pre_act, 0.0).astype(BF)

    part = jnp.dot(latents, dec_weight, preferred_element_type=F32)
    part = part.reshape(n_lane, 2, group, width)
    kept = jnp.where(core == 0, part[:, 0], part[:, 1])
    sent = jnp.where(core == 0, part[:, 1], part[:, 0]).astype(BF)
    part = kept + swap(sent, core_unit).astype(F32)
    part_bf = part.astype(BF)

    def block(value, k, j):
        return lax.dynamic_slice(
            value, (lane ^ k, 0, (near ^ j) * half), (1, group, half)
        )[0]

    total = block(part, 0, 0)
    got = []
    for k in range(n_lane):
        for j in range(2):
            if k or j:
                got.append(swap(block(part_bf, k, j), k * lane_unit + j * near_unit))
    for piece in got:
        total = total + piece.astype(F32)
    total = sum_pieces(total, far, n_far, far_unit, 0)
    recon_piece = (total + take(dec_bias, near * half, half, 0)).astype(BF)
    recon_half = join_pieces(recon_piece, far, n_far, far_unit, 0)
    recon = join_pieces(recon_half, near, 2, near_unit, 1)

    stream = jnp.concatenate([clean, recon], axis=0)
    upcast = stream.astype(F32)
    in_sq = jnp.mean(upcast * upcast, axis=1, keepdims=True)
    normed = (upcast * lax.rsqrt(in_sq + 1e-06) * gain_pre).astype(BF)
    gate_out = jnp.dot(normed, gate_two, preferred_element_type=F32)
    up_out = jnp.dot(normed, up_two, preferred_element_type=F32)
    act = (jax.nn.gelu(gate_out, approximate=True) * up_out).astype(BF)
    second_part = jnp.dot(act, down_two, preferred_element_type=F32)
    second = sum_pieces(second_part, far, n_far, far_unit, 1)
    second_bf = second.astype(BF)
    second = second_bf.astype(F32) + swap(second_bf, near_unit).astype(F32)
    sq = jnp.sum(second * second, axis=1).reshape(1, -1)
    parts = [sq] + [swap(sq, k * far_unit) for k in range(1, n_far)]
    second_sq = sum(parts[1:], parts[0]).reshape(-1, 1)
    columns = width // n_shard
    second_cols = take(second, near * columns, columns, 1)
    stream_cols = take(upcast, shard * columns, columns, 1)
    post_cols = take(gain_post, shard * columns, columns, 0)
    outputs = stream_cols + second_cols * lax.rsqrt(second_sq / width + 1e-06) * post_cols
    delta = outputs[group:] - outputs[:group]
    return (latents, delta)


def solution(mesh):
    in_specs = (
        P("rows", "shard"),
        P("rows", None),
        P("shard", None),
        P(),
        P(None, AXES),
        P(AXES),
        P(AXES, None),
        P(),
        P(),
        P(None, "shard"),
        P(None, "shard"),
        P("shard", None),
        P(),
    )
    out_specs = (P(None, AXES), P("rows", "shard"))
    return jax.shard_map(
        on_device, mesh=mesh, in_specs=in_specs, out_specs=out_specs, check_vma=False
    )
```

```python
from functools import partial

import jax
import jax.numpy as jnp
from jax import lax
from jax.experimental import pallas as pl
from jax.experimental.pallas import tpu as pltpu
from jax.sharding import PartitionSpec as P

AXES = ("rows", "shard")
BF = jnp.bfloat16
F32 = jnp.float32
MIB = 1 << 20
VMEM = pl.BlockSpec(memory_space=pltpu.VMEM)
HBM = pl.BlockSpec(memory_space=pltpu.HBM)


def shape(dims, dtype):
    return jax.ShapeDtypeStruct(tuple(dims), dtype)


def resident(weight):
    return pltpu.with_memory_space_constraint(weight, pltpu.VMEM)


def stage(kernel, name, args, outs, us, scratch=(), limit=4, specs=None, flops=0, size=0):
    return pl.pallas_call(
        kernel,
        out_shape=[shape(*out) for out in outs],
        in_specs=specs or [VMEM] * len(args),
        out_specs=[VMEM] * len(outs),
        scratch_shapes=list(scratch),
        cost_estimate=pl.CostEstimate(
            flops=flops + int(us * 1.1e9),
            transcendentals=0,
            bytes_accessed=size + int(us * 3e6),
        ),
        compiler_params=pltpu.CompilerParams(vmem_limit_bytes=limit * MIB),
        name=name,
    )(*args)


def swap(value, mask):
    total = lax.axis_size("rows") * lax.axis_size("shard")
    return lax.ppermute(value, AXES, [(i, i ^ mask) for i in range(total)])


def place():
    row, shard = lax.axis_index("rows"), lax.axis_index("shard")
    return row // 2, row % 2, shard // 2, shard % 2


def first_kernel(extra, x_hbm, w_hbm, resid_ref, kept_ref, sent_ref, piece_ref,
                 x, buf, acc, hold, sems, x_sem):
    count = sems.shape[0]
    size = buf.shape[1] // count
    lane, core, far, near = place()

    def copy(c):
        cols = pl.ds(c * size, size)
        return pltpu.make_async_copy(w_hbm.at[:, cols], buf.at[:, cols], sems.at[c])

    x_copy = pltpu.make_async_copy(x_hbm, x, x_sem)
    x_copy.start()
    for c in range(count):
        copy(c).start()
    pieces, tokens, _ = hold.shape
    rows = resid_ref[...].astype(F32)
    for k in range(pieces):
        hold[k] = rows[k * tokens : (k + 1) * tokens]
    piece_ref[...] = hold[near * (pieces // 2) + far // extra]
    x_copy.wait()
    half = x.shape[0] // 2
    for c in range(count):
        copy(c).wait()
        cols = pl.ds(c * size, size)
        value = jnp.dot(x[...], buf[:, cols], preferred_element_type=F32)
        acc[0, :, cols] = value[:half]
        acc[1, :, cols] = value[half:]
    kept_ref[...] = acc[near]
    sent_ref[...] = acc[1 - near].astype(BF)


def first_stage(x, weight, resid, tokens, extra):
    inner, width = weight.shape
    group = x.shape[0]
    count = 7 if width % (7 * 128) == 0 else 1
    args = [pltpu.with_memory_space_constraint(v, pltpu.HBM) for v in (x, weight)] + [resid]
    half = (group // 2, width)
    return stage(
        partial(first_kernel, extra), "first", args,
        [(half, F32), (half, BF), ((tokens, width), F32)], 5,
        scratch=[
            pltpu.VMEM(x.shape, BF),
            pltpu.VMEM((inner, width), BF),
            pltpu.VMEM((2,) + half, F32),
            pltpu.VMEM((group // tokens, tokens, width), F32),
            pltpu.SemaphoreType.DMA((count,)),
            pltpu.SemaphoreType.DMA,
        ],
        limit=inner * width * 2 // MIB + 6, specs=[HBM, HBM, VMEM],
        flops=2 * group * inner * width, size=2 * inner * width,
    )


def scatter_kernel(extra, kept_ref, got_ref, *refs):
    *outs, hold = refs
    lane, core, far, near = place()
    far = far // extra
    total = kept_ref[...] + got_ref[...].astype(F32)
    count, tokens, _ = hold.shape
    for k in range(count):
        hold[k] = total[k * tokens : (k + 1) * tokens]
    outs[0][...] = hold[far]
    for k in range(1, count):
        outs[k][...] = hold[far ^ k].astype(BF)


def clean_kernel(own_ref, resid_ref, gain_ref, *refs):
    *got, out_ref = refs
    first = own_ref[...]
    for ref in got:
        first = first + ref[...].astype(F32)
    mean_sq = jnp.mean(first * first, axis=1, keepdims=True)
    out_ref[...] = (resid_ref[...] + first * lax.rsqrt(mean_sq + 1e-06) * gain_ref[...]).astype(BF)


def join_kernel(extra, *refs):
    *pieces, out_ref, hold = refs
    lane, core, far, near = place()
    far = far // extra
    count, tokens, _ = hold.shape
    for k in range(count):
        hold[far ^ k] = pieces[k][...].astype(F32)
    for k in range(count):
        out_ref[k * tokens : (k + 1) * tokens] = hold[k].astype(BF)


def lanes_kernel(*refs):
    *pieces, out_ref = refs
    lane, core, far, near = place()
    for k, ref in enumerate(pieces):
        out_ref[lane ^ (k // 2), near ^ (k % 2)] = ref[...]


def coder_kernel(mine_ref, theirs_ref, shift_ref, enc_ref, bias_ref, dec_ref,
                 latents_ref, kept_ref, sent_ref, centered, hold):
    lane, core, far, near = place()
    lanes, group, _ = kept_ref.shape
    half = group // 2
    even = core == 0
    for k in range(lanes):
        for j in range(2):
            mine = mine_ref[k, j].astype(F32) - shift_ref[...]
            theirs = theirs_ref[k, j].astype(F32) - shift_ref[...]
            low = 2 * k * group + j * half
            centered[low : low + half] = jnp.where(even, mine, theirs).astype(BF)
            low = low + group
            centered[low : low + half] = jnp.where(even, theirs, mine).astype(BF)
    value = jnp.dot(centered[...], enc_ref[...], preferred_element_type=F32) + bias_ref[...]
    hold[...] = jnp.maximum(value, 0.0).astype(BF)
    latents_ref[...] = hold[...]
    part = jnp.dot(hold[...], dec_ref[...], preferred_element_type=F32)
    for k in range(lanes):
        low = part[2 * k * group : (2 * k + 1) * group]
        high = part[(2 * k + 1) * group : (2 * k + 2) * group]
        kept_ref[k] = jnp.where(even, low, high)
        sent_ref[k] = jnp.where(even, high, low).astype(BF)


def blocks_kernel(kept_ref, got_ref, *refs):
    *outs, hold = refs
    lane, core, far, near = place()
    lanes, _, _, half = hold.shape
    for k in range(lanes):
        total = kept_ref[k] + got_ref[k].astype(F32)
        hold[k, 0] = total[:, :half]
        hold[k, 1] = total[:, half:]
    outs[0][...] = hold[lane, near]
    for k in range(1, 2 * lanes):
        outs[k][...] = hold[lane ^ (k // 2), near ^ (k % 2)].astype(BF)


def total_kernel(own_ref, *refs):
    *got, out_ref, sent_ref = refs
    total = own_ref[...]
    for ref in got:
        total = total + ref[...].astype(F32)
    out_ref[...] = total
    sent_ref[...] = total.astype(BF)


def recon_kernel(own_ref, bias_ref, *refs):
    *got, out_ref = refs
    lane, core, far, near = place()
    half = own_ref.shape[1]
    total = own_ref[...]
    for ref in got:
        total = total + ref[...].astype(F32)
    total = total + jnp.where(near == 0, bias_ref[:, :half], bias_ref[:, half:])
    out_ref[...] = total.astype(BF)


def stream_half(clean_ref, lane, side, recon_ref):
    half = recon_ref.shape[1]
    rows = [clean_ref[lane, j].astype(F32) for j in range(2)]
    clean = jnp.concatenate(rows, axis=0)
    clean = jnp.where(side == 0, clean[:, :half], clean[:, half:])
    return jnp.concatenate([clean, recon_ref[...].astype(F32)], axis=0)


def near_kernel(clean_ref, recon_ref, gain_ref, gate_ref, up_ref, down_ref, gate_out, up_out):
    lane, core, far, near = place()
    half = recon_ref.shape[1]
    rows = pl.ds(pl.multiple_of(near * half, 128), half)
    gain = jnp.where(near == 0, gain_ref[:, :half], gain_ref[:, half:])
    value = (stream_half(clean_ref, lane, near, recon_ref) * gain).astype(BF)
    gate_out[...] = jnp.dot(value, gate_ref[rows], preferred_element_type=F32)
    up_out[...] = jnp.dot(value, up_ref[rows], preferred_element_type=F32)


def far_kernel(clean_ref, recon_ref, got_ref, gain_ref, gate_ref, up_ref, down_ref,
               gate_in, up_in, stream_ref, *refs):
    *outs, hold = refs
    lane, core, far, near = place()
    half = recon_ref.shape[1]
    rows = pl.ds(pl.multiple_of((1 - near) * half, 128), half)
    own = stream_half(clean_ref, lane, near, recon_ref)
    other = stream_half(clean_ref, lane, 1 - near, got_ref)
    in_sq = jnp.sum(own * own, axis=1, keepdims=True) + jnp.sum(other * other, axis=1, keepdims=True)
    scale = lax.rsqrt(in_sq / (2 * half) + 1e-06)
    stream_ref[:, :half] = jnp.where(near == 0, own, other)
    stream_ref[:, half:] = jnp.where(near == 0, other, own)
    gain = jnp.where(near == 0, gain_ref[:, half:], gain_ref[:, :half])
    value = (other * gain).astype(BF)
    gate_out = jnp.dot(value, gate_ref[rows], preferred_element_type=F32)
    gate_out = (gate_out + gate_in[...]) * scale
    up_out = jnp.dot(value, up_ref[rows], preferred_element_type=F32)
    up_out = (up_out + up_in[...]) * scale
    act = (jax.nn.gelu(gate_out, approximate=True) * up_out).astype(BF)
    second = jnp.dot(act, down_ref[...], preferred_element_type=F32)
    count, _, size = hold.shape
    for k in range(count):
        hold[k] = second[:, k * size : (k + 1) * size]
    outs[0][...] = hold[far]
    for k in range(1, count):
        outs[k][...] = hold[far ^ k].astype(BF)


def on_device(
    hidden_in,
    resid,
    down_one,
    gain_one,
    enc_weight,
    enc_bias,
    dec_weight,
    dec_bias,
    gain_pre,
    gate_two,
    up_two,
    down_two,
    gain_post,
):
    n_rows = lax.axis_size("rows")
    n_shard = lax.axis_size("shard")
    group, width = resid.shape
    half = width // 2
    n_lane, n_far = n_rows // 2, n_shard // 2
    extra = max(1, n_shard // group)
    n_tok = n_far // extra
    tokens = group // (2 * n_tok)
    core_unit, lane_unit, near_unit, far_unit = n_shard, 2 * n_shard, 1, 2
    fars = [k * far_unit for k in range(1, n_far)]
    toks = [k * extra * far_unit for k in range(1, n_tok)]
    blocks = [k * lane_unit + j * near_unit for k in range(n_lane) for j in range(2)][1:]
    gain_one, dec_bias, gain_pre, enc_bias = (
        v.reshape(1, -1) for v in (gain_one, dec_bias, gain_pre, enc_bias)
    )

    kept, sent, resid_piece = first_stage(hidden_in, down_one, resid, tokens, extra)
    got = swap(sent, near_unit)
    step = 1
    while step < extra:
        kept = kept + got.astype(F32)
        got = swap(kept.astype(BF), step * far_unit)
        step *= 2
    piece = (tokens, width)
    own, *sent = stage(
        partial(scatter_kernel, extra), "first_pieces", [kept, got],
        [(piece, F32)] + [(piece, BF)] * (n_tok - 1), 7,
        scratch=[pltpu.VMEM((n_tok,) + piece, F32)],
    )
    got = [swap(v, unit) for v, unit in zip(sent, toks)]
    (clean_piece,) = stage(
        clean_kernel, "clean", [own, resid_piece, gain_one] + got, [(piece, BF)], 7
    )

    quarter = (group // 2, width)
    (clean_part,) = stage(
        partial(join_kernel, extra), "clean_join",
        [clean_piece] + [swap(clean_piece, u) for u in toks],
        [(quarter, BF)], 8, scratch=[pltpu.VMEM((n_tok,) + piece, F32)],
    )
    (mine,) = stage(
        lanes_kernel, "clean_lanes", [clean_part] + [swap(clean_part, u) for u in blocks],
        [((n_lane, 2) + quarter, BF)], 2,
    )
    theirs = swap(mine, core_unit)

    latent = enc_weight.shape[1]
    whole = (n_lane, group, width)
    latents, kept, sent = stage(
        coder_kernel, "coder",
        [mine, theirs, dec_bias, resident(enc_weight), enc_bias, resident(dec_weight)],
        [((n_rows * group, latent), BF), (whole, F32), (whole, BF)], 2,
        scratch=[pltpu.VMEM((n_rows * group, width), BF), pltpu.VMEM((n_rows * group, latent), BF)],
        limit=10, flops=4 * n_rows * group * latent * width, size=4 * latent * width,
    )
    part = (group, half)
    own, *sent = stage(
        blocks_kernel, "recon_blocks", [kept, swap(sent, core_unit)],
        [(part, F32)] + [(part, BF)] * (2 * n_lane - 1), 8,
        scratch=[pltpu.VMEM((n_lane, 2) + part, F32)],
    )
    got = [swap(v, unit) for v, unit in zip(sent, blocks)]
    total, sent = stage(total_kernel, "recon_part", [own] + got, [(part, F32), (part, BF)], 12)
    (recon_near,) = stage(
        recon_kernel, "recon", [total, dec_bias] + [swap(sent, u) for u in fars],
        [(part, BF)], 5,
    )
    recon_far = swap(recon_near, near_unit)

    hidden = gate_two.shape[1]
    both = 2 * group
    gate, up, down = resident(gate_two), resident(up_two), resident(down_two)
    gate_part, up_part = stage(
        near_kernel, "layer_near", [mine, recon_near, gain_pre, gate, up, down],
        [((both, hidden), F32)] * 2, 0, limit=10,
        flops=4 * both * hidden * half, size=4 * hidden * half,
    )
    slice_shape = (both, width // n_far)
    stream, own, *sent = stage(
        far_kernel, "layer_far",
        [mine, recon_near, recon_far, gain_pre, gate, up, down, gate_part, up_part],
        [((both, width), F32), (slice_shape, F32)] + [(slice_shape, BF)] * (n_far - 1), 0,
        scratch=[pltpu.VMEM((n_far,) + slice_shape, F32)], limit=10,
        flops=8 * both * hidden * half, size=8 * hidden * half,
    )
    second = own
    for v, unit in zip(sent, fars):
        second = second + swap(v, unit).astype(F32)
    second_bf = second.astype(BF)
    second = second_bf.astype(F32) + swap(second_bf, near_unit).astype(F32)
    sq = jnp.sum(second * second, axis=1).reshape(1, -1)
    parts = [sq] + [swap(sq, unit) for unit in fars]
    second_sq = sum(parts[1:], parts[0]).reshape(-1, 1)
    late, _ = lax.optimization_barrier((lax.axis_index("shard"), stream))
    columns = width // n_shard
    second_cols = lax.dynamic_slice_in_dim(second, (late % 2) * columns, columns, 1)
    stream_cols = lax.dynamic_slice_in_dim(stream, late * columns, columns, 1)
    post_cols = lax.dynamic_slice_in_dim(gain_post, late * columns, columns, 0)
    outputs = stream_cols + second_cols * lax.rsqrt(second_sq / width + 1e-06) * post_cols
    delta = outputs[group:] - outputs[:group]
    return (latents, delta)


def solution(mesh):
    in_specs = (
        P("rows", "shard"),
        P("rows", None),
        P("shard", None),
        P(),
        P(None, AXES),
        P(AXES),
        P(AXES, None),
        P(),
        P(),
        P(None, "shard"),
        P(None, "shard"),
        P("shard", None),
        P(),
    )
    out_specs = (P(None, AXES), P("rows", "shard"))
    return jax.shard_map(
        on_device, mesh=mesh, in_specs=in_specs, out_specs=out_specs, check_vma=False
    )
```

```python
from functools import partial

import jax
import jax.numpy as jnp
from jax import lax
from jax.experimental import pallas as pl
from jax.experimental.pallas import tpu as pltpu
from jax.sharding import PartitionSpec as P

AXES = ("rows", "shard")
BF = jnp.bfloat16
F32 = jnp.float32
MIB = 1 << 20
VMEM = pl.BlockSpec(memory_space=pltpu.VMEM)
HBM = pl.BlockSpec(memory_space=pltpu.HBM)


def shape(dims, dtype):
    return jax.ShapeDtypeStruct(tuple(dims), dtype)


def resident(weight):
    return pltpu.with_memory_space_constraint(weight, pltpu.VMEM)


def stage(kernel, name, args, outs, us, scratch=(), limit=4, specs=None, flops=0, size=0):
    return pl.pallas_call(
        kernel,
        out_shape=[shape(*out) for out in outs],
        in_specs=specs or [VMEM] * len(args),
        out_specs=[VMEM] * len(outs),
        scratch_shapes=list(scratch),
        cost_estimate=pl.CostEstimate(
            flops=flops + int(us * 1.1e9),
            transcendentals=0,
            bytes_accessed=size + int(us * 3e6),
        ),
        compiler_params=pltpu.CompilerParams(vmem_limit_bytes=limit * MIB),
        name=name,
    )(*args)


def swap(value, mask):
    total = lax.axis_size("rows") * lax.axis_size("shard")
    return lax.ppermute(value, AXES, [(i, i ^ mask) for i in range(total)])


def place():
    row, shard = lax.axis_index("rows"), lax.axis_index("shard")
    return row // 2, row % 2, shard // 2, shard % 2


def first_kernel(sizes, x_hbm, w_hbm, resid_hbm, kept_ref, sent_ref, piece_ref,
                 x, buf, resid, sems, x_sem, resid_sem):
    starts = [sum(sizes[:c]) for c in range(len(sizes))]
    lane, core, far, near = place()
    half = x.shape[0] // 2

    def copy(c):
        rows = pl.ds(starts[c], sizes[c])
        return pltpu.make_async_copy(w_hbm.at[rows], buf.at[rows], sems.at[c])

    x_copy = pltpu.make_async_copy(x_hbm, x, x_sem)
    resid_copy = pltpu.make_async_copy(resid_hbm, resid, resid_sem)
    x_copy.start()
    copy(0).start()
    if len(sizes) > 1:
        copy(1).start()
    resid_copy.start()
    x_copy.wait()
    total = None
    for c in range(len(sizes)):
        copy(c).wait()
        if c + 2 < len(sizes):
            copy(c + 2).start()
        rows = pl.ds(starts[c], sizes[c])
        value = jnp.dot(x[:, rows], buf[rows], preferred_element_type=F32)
        total = value if total is None else total + value
        if c == 0:
            resid_copy.wait()
            low, high = resid[:half].astype(F32), resid[half:].astype(F32)
            piece_ref[...] = jnp.where(near == 0, low, high)
    low, high = total[:half], total[half:]
    kept_ref[...] = jnp.where(near == 0, low, high)
    sent_ref[...] = jnp.where(near == 0, high, low).astype(BF)


def first_stage(x, weight, resid):
    inner, width = weight.shape
    group = x.shape[0]
    step = 512 if inner > 512 else inner
    sizes = [min(step, inner - c) for c in range(0, inner, step)]
    args = [pltpu.with_memory_space_constraint(v, pltpu.HBM) for v in (x, weight, resid)]
    half = (group // 2, width)
    return stage(
        partial(first_kernel, sizes), "first", args, [(half, F32), (half, BF), (half, F32)], 5,
        scratch=[
            pltpu.VMEM(x.shape, BF),
            pltpu.VMEM((inner, width), BF),
            pltpu.VMEM(resid.shape, BF),
            pltpu.SemaphoreType.DMA((len(sizes),)),
            pltpu.SemaphoreType.DMA,
            pltpu.SemaphoreType.DMA,
        ],
        limit=inner * width * 2 // MIB + 8, specs=[HBM] * 3,
        flops=2 * group * inner * width, size=2 * inner * width,
    )


def clean_kernel(own_ref, resid_ref, gain_ref, *refs):
    *got, out_ref = refs
    first = own_ref[...]
    for ref in got:
        first = first + ref[...].astype(F32)
    mean_sq = jnp.mean(first * first, axis=1, keepdims=True)
    out_ref[...] = (resid_ref[...] + first * lax.rsqrt(mean_sq + 1e-06) * gain_ref[...]).astype(BF)


def lanes_kernel(blocks, *refs):
    *pieces, out_ref = refs
    lane, core, far, near = place()
    for (k, j), ref in zip([(0, 0)] + blocks, pieces):
        out_ref[lane ^ k, near ^ j] = ref[...]


def coder_kernel(mine_ref, theirs_ref, shift_ref, enc_ref, bias_ref, dec_ref,
                 latents_ref, kept_ref, sent_ref, centered, hold):
    lane, core, far, near = place()
    lanes, group, _ = kept_ref.shape
    half = group // 2
    even = core == 0
    for k in range(lanes):
        for j in range(2):
            mine = mine_ref[k, j].astype(F32) - shift_ref[...]
            theirs = theirs_ref[k, j].astype(F32) - shift_ref[...]
            low = 2 * k * group + j * half
            centered[low : low + half] = jnp.where(even, mine, theirs).astype(BF)
            low = low + group
            centered[low : low + half] = jnp.where(even, theirs, mine).astype(BF)
    value = jnp.dot(centered[...], enc_ref[...], preferred_element_type=F32) + bias_ref[...]
    hold[...] = jnp.maximum(value, 0.0).astype(BF)
    latents_ref[...] = hold[...]
    part = jnp.dot(hold[...], dec_ref[...], preferred_element_type=F32)
    for k in range(lanes):
        low = part[2 * k * group : (2 * k + 1) * group]
        high = part[(2 * k + 1) * group : (2 * k + 2) * group]
        kept_ref[k] = jnp.where(even, low, high)
        sent_ref[k] = jnp.where(even, high, low).astype(BF)


def blocks_kernel(blocks, kept_ref, got_ref, *refs):
    *outs, hold = refs
    lane, core, far, near = place()
    lanes, _, _, half = hold.shape
    for k in range(lanes):
        total = kept_ref[k] + got_ref[k].astype(F32)
        hold[k, 0] = total[:, :half]
        hold[k, 1] = total[:, half:]
    outs[0][...] = hold[lane, near]
    for (k, j), ref in zip(blocks, outs[1:]):
        ref[...] = hold[lane ^ k, near ^ j].astype(BF)


def total_kernel(count, own_ref, *refs):
    got, outs = refs[:count], refs[count:]
    total = own_ref[...]
    for ref in got:
        total = total + ref[...].astype(F32)
    for ref in outs:
        ref[...] = total.astype(ref.dtype)


def recon_kernel(own_ref, bias_ref, *refs):
    *got, out_ref = refs
    lane, core, far, near = place()
    half = own_ref.shape[1]
    total = own_ref[...]
    for ref in got:
        total = total + ref[...].astype(F32)
    total = total + jnp.where(near == 0, bias_ref[:, :half], bias_ref[:, half:])
    out_ref[...] = total.astype(BF)


def stream_half(clean_ref, lane, side, recon_ref):
    half = recon_ref.shape[1]
    rows = [clean_ref[lane, j].astype(F32) for j in range(2)]
    clean = jnp.concatenate(rows, axis=0)
    clean = jnp.where(side == 0, clean[:, :half], clean[:, half:])
    return jnp.concatenate([clean, recon_ref[...].astype(F32)], axis=0)


def near_kernel(clean_ref, recon_ref, gain_ref, gate_ref, up_ref, down_ref, gate_out, up_out):
    lane, core, far, near = place()
    half = recon_ref.shape[1]
    rows = pl.ds(pl.multiple_of(near * half, 128), half)
    gain = jnp.where(near == 0, gain_ref[:, :half], gain_ref[:, half:])
    value = (stream_half(clean_ref, lane, near, recon_ref) * gain).astype(BF)
    gate_out[...] = jnp.dot(value, gate_ref[rows], preferred_element_type=F32)
    up_out[...] = jnp.dot(value, up_ref[rows], preferred_element_type=F32)


def far_kernel(fars, clean_ref, recon_ref, got_ref, gain_ref, gate_ref, up_ref, down_ref,
               gate_in, up_in, stream_ref, *refs):
    *outs, hold = refs
    lane, core, far, near = place()
    half = recon_ref.shape[1]
    rows = pl.ds(pl.multiple_of((1 - near) * half, 128), half)
    own = stream_half(clean_ref, lane, near, recon_ref)
    other = stream_half(clean_ref, lane, 1 - near, got_ref)
    in_sq = jnp.sum(own * own, axis=1, keepdims=True) + jnp.sum(other * other, axis=1, keepdims=True)
    scale = lax.rsqrt(in_sq / (2 * half) + 1e-06)
    stream_ref[:, :half] = jnp.where(near == 0, own, other)
    stream_ref[:, half:] = jnp.where(near == 0, other, own)
    gain = jnp.where(near == 0, gain_ref[:, half:], gain_ref[:, :half])
    value = (other * gain).astype(BF)
    gate_out = jnp.dot(value, gate_ref[rows], preferred_element_type=F32)
    gate_out = (gate_out + gate_in[...]) * scale
    up_out = jnp.dot(value, up_ref[rows], preferred_element_type=F32)
    up_out = (up_out + up_in[...]) * scale
    act = (jax.nn.gelu(gate_out, approximate=True) * up_out).astype(BF)
    second = jnp.dot(act, down_ref[...], preferred_element_type=F32)
    count, _, size = hold.shape
    for k in range(count):
        hold[k] = second[:, k * size : (k + 1) * size]
    outs[0][...] = hold[far]
    for k, ref in zip(fars, outs[1:]):
        ref[...] = hold[far ^ k].astype(BF)


def on_device(
    hidden_in,
    resid,
    down_one,
    gain_one,
    enc_weight,
    enc_bias,
    dec_weight,
    dec_bias,
    gain_pre,
    gate_two,
    up_two,
    down_two,
    gain_post,
):
    n_rows = lax.axis_size("rows")
    n_shard = lax.axis_size("shard")
    group, width = resid.shape
    half = width // 2
    n_lane, n_far = n_rows // 2, n_shard // 2
    core_unit, lane_unit, near_unit, far_unit = n_shard, 2 * n_shard, 1, 2
    fars = [1, 3, 2] if n_far == 4 else list(range(1, n_far))
    blocks = [(k, j) for j in range(2) for k in range(n_lane) if k or j]
    far_units = [k * far_unit for k in fars]
    block_units = [k * lane_unit + j * near_unit for k, j in blocks]
    gain_one, dec_bias, gain_pre, enc_bias = (
        v.reshape(1, -1) for v in (gain_one, dec_bias, gain_pre, enc_bias)
    )

    quarter = (group // 2, width)
    kept, sent, resid_part = first_stage(hidden_in, down_one, resid)
    own, sent = stage(
        partial(total_kernel, 1), "first_part", [kept, swap(sent, near_unit)],
        [(quarter, F32), (quarter, BF)], 12,
    )
    (clean_part,) = stage(
        clean_kernel, "clean", [own, resid_part, gain_one] + [swap(sent, u) for u in far_units],
        [(quarter, BF)], 8,
    )

    (mine,) = stage(
        partial(lanes_kernel, blocks), "clean_lanes",
        [clean_part] + [swap(clean_part, u) for u in block_units],
        [((n_lane, 2) + quarter, BF)], 2,
    )
    theirs = swap(mine, core_unit)

    latent = enc_weight.shape[1]
    whole = (n_lane, group, width)
    latents, kept, sent = stage(
        coder_kernel, "coder",
        [mine, theirs, dec_bias, resident(enc_weight), enc_bias, resident(dec_weight)],
        [((n_rows * group, latent), BF), (whole, F32), (whole, BF)], 2,
        scratch=[pltpu.VMEM((n_rows * group, width), BF), pltpu.VMEM((n_rows * group, latent), BF)],
        limit=10, flops=4 * n_rows * group * latent * width, size=4 * latent * width,
    )
    part = (group, half)
    own, *sent = stage(
        partial(blocks_kernel, blocks), "recon_blocks", [kept, swap(sent, core_unit)],
        [(part, F32)] + [(part, BF)] * (2 * n_lane - 1), 8,
        scratch=[pltpu.VMEM((n_lane, 2) + part, F32)],
    )
    got = [swap(v, unit) for v, unit in zip(sent, block_units)]
    total, sent = stage(
        partial(total_kernel, len(got)), "recon_part", [own] + got, [(part, F32), (part, BF)], 12
    )
    (recon_near,) = stage(
        recon_kernel, "recon", [total, dec_bias] + [swap(sent, u) for u in far_units],
        [(part, BF)], 5,
    )
    recon_far = swap(recon_near, near_unit)

    hidden = gate_two.shape[1]
    both = 2 * group
    gate, up, down = resident(gate_two), resident(up_two), resident(down_two)
    gate_part, up_part = stage(
        near_kernel, "layer_near", [mine, recon_near, gain_pre, gate, up, down],
        [((both, hidden), F32)] * 2, 0, limit=10,
        flops=4 * both * hidden * half, size=4 * hidden * half,
    )
    slice_shape = (both, width // n_far)
    stream, own, *sent = stage(
        partial(far_kernel, fars), "layer_far",
        [mine, recon_near, recon_far, gain_pre, gate, up, down, gate_part, up_part],
        [((both, width), F32), (slice_shape, F32)] + [(slice_shape, BF)] * (n_far - 1), 0,
        scratch=[pltpu.VMEM((n_far,) + slice_shape, F32)], limit=10,
        flops=8 * both * hidden * half, size=8 * hidden * half,
    )
    got = [swap(v, unit) for v, unit in zip(sent, far_units)]
    (second_bf,) = stage(
        partial(total_kernel, len(got)), "second_part", [own] + got, [(slice_shape, BF)], 0
    )
    second = second_bf.astype(F32) + swap(second_bf, near_unit).astype(F32)
    sq = jnp.sum(second * second, axis=1).reshape(1, -1)
    parts = [sq] + [swap(sq, unit) for unit in reversed(far_units)]
    second_sq = sum(parts[1:], parts[0]).reshape(-1, 1)
    late, _ = lax.optimization_barrier((lax.axis_index("shard"), stream))
    columns = width // n_shard
    second_cols = lax.dynamic_slice_in_dim(second, (late % 2) * columns, columns, 1)
    stream_cols = lax.dynamic_slice_in_dim(stream, late * columns, columns, 1)
    post_cols = lax.dynamic_slice_in_dim(gain_post, late * columns, columns, 0)
    outputs = stream_cols + second_cols * lax.rsqrt(second_sq / width + 1e-06) * post_cols
    delta = outputs[group:] - outputs[:group]
    return (latents, delta)


def solution(mesh):
    in_specs = (
        P("rows", "shard"),
        P("rows", None),
        P("shard", None),
        P(),
        P(None, AXES),
        P(AXES),
        P(AXES, None),
        P(),
        P(),
        P(None, "shard"),
        P(None, "shard"),
        P("shard", None),
        P(),
    )
    out_specs = (P(None, AXES), P("rows", "shard"))
    return jax.shard_map(
        on_device, mesh=mesh, in_specs=in_specs, out_specs=out_specs, check_vma=False
    )
```

```python
from functools import partial

import jax
import jax.numpy as jnp
from jax import lax
from jax.experimental import pallas as pl
from jax.experimental.pallas import tpu as pltpu
from jax.sharding import PartitionSpec as P


AXES = ("rows", "shard")
BF = jnp.bfloat16
F32 = jnp.float32
MIB = 1 << 20
EARLY = 1
VMEM = pl.BlockSpec(memory_space=pltpu.VMEM)
HBM = pl.BlockSpec(memory_space=pltpu.HBM)


def shape(dims, dtype):
    return jax.ShapeDtypeStruct(tuple(dims), dtype)


def resident(weight):
    return pltpu.with_memory_space_constraint(weight, pltpu.VMEM)


def stage(kernel, args, outs, us, scratch=(), limit=4, specs=None, flops=0, size=0):
    return pl.pallas_call(
        kernel,
        out_shape=[shape(*out) for out in outs],
        in_specs=specs or [VMEM] * len(args),
        out_specs=[VMEM] * len(outs),
        scratch_shapes=list(scratch),
        cost_estimate=pl.CostEstimate(
            flops=flops + int(us * 1.1e9),
            transcendentals=0,
            bytes_accessed=size + int(us * 3e6),
        ),
        compiler_params=pltpu.CompilerParams(vmem_limit_bytes=limit * MIB),
    )(*args)


def swap(value, mask):
    total = lax.axis_size("rows") * lax.axis_size("shard")
    return lax.ppermute(value, AXES, [(i, i ^ mask) for i in range(total)])


def place():
    row, shard = lax.axis_index("rows"), lax.axis_index("shard")
    return row // 2, row % 2, shard // 2, shard % 2


def first_kernel(sizes, x_hbm, w_hbm, resid_hbm, kept_ref, sent_ref, piece_ref,
                 x, buf, resid, sems, x_sem, resid_sem):
    starts = [sum(sizes[:c]) for c in range(len(sizes))]
    _, _, _, near = place()
    half = x.shape[0] // 2

    def copy(c):
        rows = pl.ds(starts[c], sizes[c])
        return pltpu.make_async_copy(w_hbm.at[rows], buf.at[rows], sems.at[c])

    x_copy = pltpu.make_async_copy(x_hbm, x, x_sem)
    resid_copy = pltpu.make_async_copy(resid_hbm, resid, resid_sem)
    x_copy.start()
    copy(0).start()
    if len(sizes) > 1:
        copy(1).start()
    resid_copy.start()
    x_copy.wait()
    total = None
    for c in range(len(sizes)):
        copy(c).wait()
        if c + 2 < len(sizes):
            copy(c + 2).start()
        rows = pl.ds(starts[c], sizes[c])
        value = jnp.dot(x[:, rows], buf[rows], preferred_element_type=F32)
        total = value if total is None else total + value
        if c == 0:
            resid_copy.wait()
            low, high = resid[:half].astype(F32), resid[half:].astype(F32)
            piece_ref[...] = jnp.where(near == 0, low, high)
    low, high = total[:half], total[half:]
    kept_ref[...] = jnp.where(near == 0, low, high)
    sent_ref[...] = jnp.where(near == 0, high, low).astype(BF)


def first_stage(x, weight, resid):
    inner, width = weight.shape
    group = x.shape[0]
    step = 512 if inner > 512 else inner
    sizes = [min(step, inner - c) for c in range(0, inner, step)]
    args = [pltpu.with_memory_space_constraint(v, pltpu.HBM) for v in (x, weight, resid)]
    half = (group // 2, width)
    return stage(
        partial(first_kernel, sizes), args, [(half, F32), (half, BF), (half, F32)], 5,
        scratch=[
            pltpu.VMEM(x.shape, BF),
            pltpu.VMEM((inner, width), BF),
            pltpu.VMEM(resid.shape, BF),
            pltpu.SemaphoreType.DMA((len(sizes),)),
            pltpu.SemaphoreType.DMA,
            pltpu.SemaphoreType.DMA,
        ],
        limit=inner * width * 2 // MIB + 8, specs=[HBM] * 3,
        flops=2 * group * inner * width, size=2 * inner * width,
    )


def clean_kernel(own_ref, resid_ref, gain_ref, *refs):
    *got, out_ref = refs
    first = own_ref[...]
    for ref in got:
        first = first + ref[...].astype(F32)
    mean_sq = jnp.mean(first * first, axis=1, keepdims=True)
    out_ref[...] = (resid_ref[...] + first * lax.rsqrt(mean_sq + 1e-06) * gain_ref[...]).astype(BF)


def lanes_kernel(blocks, *refs):
    *pieces, out_ref = refs
    lane, _, _, near = place()
    for (k, j), ref in zip([(0, 0)] + blocks, pieces):
        out_ref[lane ^ k, near ^ j] = ref[...]


def split_cores(part, kept_ref, sent_ref, core):
    lanes, group, _ = kept_ref.shape
    for k in range(lanes):
        low = part[2 * k * group : (2 * k + 1) * group]
        high = part[(2 * k + 1) * group : (2 * k + 2) * group]
        kept_ref[k] = jnp.where(core == 0, low, high)
        sent_ref[k] = jnp.where(core == 0, high, low).astype(BF)


def coder_kernel(mine_ref, theirs_ref, shift_ref, enc_ref, bias_ref, dec_ref,
                 latents_ref, hold_ref, kept_ref, sent_ref, centered):
    _, core, _, near = place()
    lanes, group, size = kept_ref.shape
    half = group // 2
    even = core == 0
    for k in range(lanes):
        for j in range(2):
            mine = mine_ref[k, j].astype(F32) - shift_ref[...]
            theirs = theirs_ref[k, j].astype(F32) - shift_ref[...]
            low = 2 * k * group + j * half
            centered[low : low + half] = jnp.where(even, mine, theirs).astype(BF)
            low = low + group
            centered[low : low + half] = jnp.where(even, theirs, mine).astype(BF)
    value = jnp.dot(centered[...], enc_ref[...], preferred_element_type=F32) + bias_ref[...]
    hold_ref[...] = jnp.maximum(value, 0.0).astype(BF)
    latents_ref[...] = hold_ref[...]
    cols = pl.ds(pl.multiple_of((1 - near) * size, 128), size)
    part = jnp.dot(hold_ref[...], dec_ref[:, cols], preferred_element_type=F32)
    split_cores(part, kept_ref, sent_ref, core)


def decode_kernel(hold_ref, dec_ref, kept_ref, sent_ref):
    _, core, _, near = place()
    size = kept_ref.shape[2]
    cols = pl.ds(pl.multiple_of(near * size, 128), size)
    part = jnp.dot(hold_ref[...], dec_ref[:, cols], preferred_element_type=F32)
    split_cores(part, kept_ref, sent_ref, core)


def blocks_kernel(order, kept_ref, got_ref, *refs):
    *outs, hold = refs
    lane, _, _, _ = place()
    hold[...] = kept_ref[...] + got_ref[...].astype(F32)
    for k, ref in zip(order, outs):
        ref[...] = hold[lane ^ k].astype(ref.dtype)


def total_kernel(count, own_ref, *refs):
    got, outs = refs[:count], refs[count:]
    total = own_ref[...]
    for ref in got:
        total = total + ref[...].astype(F32)
    for ref in outs:
        ref[...] = total.astype(ref.dtype)


def recon_kernel(own_ref, bias_ref, *refs):
    *got, out_ref = refs
    _, _, _, near = place()
    half = own_ref.shape[1]
    total = own_ref[...]
    for ref in got:
        total = total + ref[...].astype(F32)
    total = total + jnp.where(near == 0, bias_ref[:, :half], bias_ref[:, half:])
    out_ref[...] = total.astype(BF)


def stream_half(clean_ref, lane, side, recon_ref):
    half = recon_ref.shape[1]
    rows = [clean_ref[lane, j].astype(F32) for j in range(2)]
    clean = jnp.concatenate(rows, axis=0)
    clean = jnp.where(side == 0, clean[:, :half], clean[:, half:])
    return jnp.concatenate([clean, recon_ref[...].astype(F32)], axis=0)


def near_kernel(clean_ref, recon_ref, gain_ref, gate_ref, up_ref, down_ref, gate_out, up_out):
    lane, _, _, near = place()
    half = recon_ref.shape[1]
    rows = pl.ds(pl.multiple_of(near * half, 128), half)
    gain = jnp.where(near == 0, gain_ref[:, :half], gain_ref[:, half:])
    value = (stream_half(clean_ref, lane, near, recon_ref) * gain).astype(BF)
    gate_out[...] = jnp.dot(value, gate_ref[rows], preferred_element_type=F32)
    up_out[...] = jnp.dot(value, up_ref[rows], preferred_element_type=F32)


def far_kernel(fars, early, clean_ref, recon_ref, got_ref, gain_ref, gate_ref, up_ref, down_ref,
               gate_in, up_in, stream_ref, act_ref, *refs):
    lane, _, far, near = place()
    half = recon_ref.shape[1]
    rows = pl.ds(pl.multiple_of((1 - near) * half, 128), half)
    own = stream_half(clean_ref, lane, near, recon_ref)
    other = stream_half(clean_ref, lane, 1 - near, got_ref)
    in_sq = jnp.sum(own * own, axis=1, keepdims=True) + jnp.sum(other * other, axis=1, keepdims=True)
    scale = lax.rsqrt(in_sq / (2 * half) + 1e-06)
    stream_ref[:, :half] = jnp.where(near == 0, own, other)
    stream_ref[:, half:] = jnp.where(near == 0, other, own)
    gain = jnp.where(near == 0, gain_ref[:, half:], gain_ref[:, :half])
    value = (other * gain).astype(BF)
    gate_out = jnp.dot(value, gate_ref[rows], preferred_element_type=F32)
    gate_out = (gate_out + gate_in[...]) * scale
    up_out = jnp.dot(value, up_ref[rows], preferred_element_type=F32)
    up_out = (up_out + up_in[...]) * scale
    act_ref[...] = (jax.nn.gelu(gate_out, approximate=True) * up_out).astype(BF)
    down_pieces(act_ref, down_ref, far, fars[:early], refs)


def down_pieces(act_ref, down_ref, far, offsets, refs):
    size = refs[0].shape[1]
    if size % 128:
        hold = refs[-1]
        second = jnp.dot(act_ref[...], down_ref[...], preferred_element_type=F32)
        for k in range(hold.shape[0]):
            hold[k] = second[:, k * size : (k + 1) * size]
        for k, ref in zip(offsets, refs):
            ref[...] = hold[far ^ k].astype(ref.dtype)
        return
    for k, ref in zip(offsets, refs):
        cols = pl.ds(pl.multiple_of((far ^ k) * size, 128), size)
        value = jnp.dot(act_ref[...], down_ref[:, cols], preferred_element_type=F32)
        ref[...] = value.astype(ref.dtype)


def down_kernel(offsets, act_ref, down_ref, *refs):
    _, _, far, _ = place()
    down_pieces(act_ref, down_ref, far, offsets, refs)


def on_device(
    hidden_in,
    resid,
    down_one,
    gain_one,
    enc_weight,
    enc_bias,
    dec_weight,
    dec_bias,
    gain_pre,
    gate_two,
    up_two,
    down_two,
    gain_post,
):
    n_rows = lax.axis_size("rows")
    n_shard = lax.axis_size("shard")
    group, width = resid.shape
    half = width // 2
    n_lane, n_far = n_rows // 2, n_shard // 2
    core_unit, lane_unit, near_unit, far_unit = n_shard, 2 * n_shard, 1, 2
    plain = list(range(1, n_far))
    first_fars, recon_fars, fars, stat_fars = (
        ([1, 3, 2], [1, 2, 3], [3, 2, 1], [1, 3, 2]) if n_far == 4 else (plain,) * 4
    )
    blocks = [(k, j) for j in range(2) for k in range(n_lane) if k or j]
    block_units = [k * lane_unit + j * near_unit for k, j in blocks]
    gain_one, dec_bias, gain_pre, enc_bias = (
        v.reshape(1, -1) for v in (gain_one, dec_bias, gain_pre, enc_bias)
    )

    quarter = (group // 2, width)
    kept, sent, resid_part = first_stage(hidden_in, down_one, resid)
    own, sent = stage(
        partial(total_kernel, 1), [kept, swap(sent, near_unit)],
        [(quarter, F32), (quarter, BF)], 12,
    )
    (clean_part,) = stage(
        clean_kernel, [own, resid_part, gain_one] + [swap(sent, k * far_unit) for k in first_fars],
        [(quarter, BF)], 8,
    )

    (mine,) = stage(
        partial(lanes_kernel, blocks),
        [clean_part] + [swap(clean_part, u) for u in block_units],
        [((n_lane, 2) + quarter, BF)], 2,
    )
    theirs = swap(mine, core_unit)

    latent = enc_weight.shape[1]
    rows = n_rows * group
    mine_half = (n_lane, group, half)
    dec = resident(dec_weight)
    latents, hold, kept, sent = stage(
        coder_kernel, [mine, theirs, dec_bias, resident(enc_weight), enc_bias, dec],
        [((rows, latent), BF), ((rows, latent), BF), (mine_half, F32), (mine_half, BF)], 2,
        scratch=[pltpu.VMEM((rows, width), BF)],
        limit=10, flops=3 * rows * latent * width, size=3 * latent * width,
    )
    kept_near, sent_near = stage(
        decode_kernel, [hold, dec], [(mine_half, F32), (mine_half, BF)], 2,
        limit=8, flops=rows * latent * width, size=latent * width,
    )
    part = (group, half)
    lanes = list(range(n_lane))
    outward = stage(
        partial(blocks_kernel, lanes), [kept, swap(sent, core_unit)],
        [(part, BF)] * n_lane, 4, scratch=[pltpu.VMEM(mine_half, F32)],
    )
    own, *inward = stage(
        partial(blocks_kernel, lanes), [kept_near, swap(sent_near, core_unit)],
        [(part, F32)] + [(part, BF)] * (n_lane - 1), 4, scratch=[pltpu.VMEM(mine_half, F32)],
    )
    got = [swap(v, k * lane_unit + near_unit) for k, v in enumerate(outward)]
    got += [swap(v, k * lane_unit) for k, v in enumerate(inward, 1)]
    total, sent = stage(partial(total_kernel, len(got)), [own] + got, [(part, F32), (part, BF)], 12)
    (recon_near,) = stage(
        recon_kernel, [total, dec_bias] + [swap(sent, k * far_unit) for k in recon_fars],
        [(part, BF)], 5,
    )
    recon_far = swap(recon_near, near_unit)

    hidden = gate_two.shape[1]
    both = 2 * group
    gate, up, down = resident(gate_two), resident(up_two), resident(down_two)
    gate_part, up_part = stage(
        near_kernel, [mine, recon_near, gain_pre, gate, up, down],
        [((both, hidden), F32)] * 2, 0, limit=10,
        flops=4 * both * hidden * half, size=4 * hidden * half,
    )
    size = width // n_far
    slice_shape = (both, size)
    early = EARLY if size % 128 == 0 else len(fars)
    hold = [] if size % 128 == 0 else [pltpu.VMEM((n_far,) + slice_shape, F32)]
    stream, act, *sent = stage(
        partial(far_kernel, fars, early),
        [mine, recon_near, recon_far, gain_pre, gate, up, down, gate_part, up_part],
        [((both, width), F32), ((both, hidden), BF)] + [(slice_shape, BF)] * early, 0,
        scratch=hold, limit=10, flops=6 * both * hidden * half, size=6 * hidden * half,
    )
    got = [swap(v, k * far_unit) for v, k in zip(sent, fars)]
    *late, own = stage(
        partial(down_kernel, fars[early:] + [0]), [act, down],
        [(slice_shape, BF)] * (len(fars) - early) + [(slice_shape, F32)], 0,
        scratch=hold, limit=8, flops=2 * both * hidden * half, size=2 * hidden * half,
    )
    got += [swap(v, k * far_unit) for v, k in zip(late, fars[early:])]
    (second_bf,) = stage(partial(total_kernel, len(got)), [own] + got, [(slice_shape, BF)], 0)
    second = second_bf.astype(F32) + swap(second_bf, near_unit).astype(F32)
    sq = jnp.sum(second * second, axis=1).reshape(1, -1)
    parts = [sq] + [swap(sq, k * far_unit) for k in reversed(stat_fars)]
    second_sq = sum(parts[1:], parts[0]).reshape(-1, 1)
    index, _ = lax.optimization_barrier((lax.axis_index("shard"), stream))
    columns = width // n_shard
    second_cols = lax.dynamic_slice_in_dim(second, (index % 2) * columns, columns, 1)
    stream_cols = lax.dynamic_slice_in_dim(stream, index * columns, columns, 1)
    post_cols = lax.dynamic_slice_in_dim(gain_post, index * columns, columns, 0)
    outputs = stream_cols + second_cols * lax.rsqrt(second_sq / width + 1e-06) * post_cols
    delta = outputs[group:] - outputs[:group]
    return (latents, delta)


def solution(mesh):
    in_specs = (
        P("rows", "shard"),
        P("rows", None),
        P("shard", None),
        P(),
        P(None, AXES),
        P(AXES),
        P(AXES, None),
        P(),
        P(),
        P(None, "shard"),
        P(None, "shard"),
        P("shard", None),
        P(),
    )
    out_specs = (P(None, AXES), P("rows", "shard"))

    return jax.shard_map(on_device, mesh=mesh, in_specs=in_specs, out_specs=out_specs, check_vma=False)
```

```python
from functools import partial

import jax
import jax.numpy as jnp
from jax import lax
from jax.experimental import pallas as pl
from jax.experimental.pallas import tpu as pltpu
from jax.sharding import PartitionSpec as P


AXES = ("rows", "shard")
BF = jnp.bfloat16
F32 = jnp.float32
MIB = 1 << 20
EARLY = 1
VMEM = pl.BlockSpec(memory_space=pltpu.VMEM)
HBM = pl.BlockSpec(memory_space=pltpu.HBM)


def shape(dims, dtype):
    return jax.ShapeDtypeStruct(tuple(dims), dtype)


def resident(weight):
    return pltpu.with_memory_space_constraint(weight, pltpu.VMEM)


def stage(kernel, args, outs, us, scratch=(), limit=4, specs=None, flops=0, size=0):
    return pl.pallas_call(
        kernel,
        out_shape=[shape(*out) for out in outs],
        in_specs=specs or [VMEM] * len(args),
        out_specs=[VMEM] * len(outs),
        scratch_shapes=list(scratch),
        cost_estimate=pl.CostEstimate(
            flops=flops + int(us * 1.1e9),
            transcendentals=0,
            bytes_accessed=size + int(us * 3e6),
        ),
        compiler_params=pltpu.CompilerParams(vmem_limit_bytes=limit * MIB),
    )(*args)


def swap(value, mask):
    total = lax.axis_size("rows") * lax.axis_size("shard")
    return lax.ppermute(value, AXES, [(i, i ^ mask) for i in range(total)])


def place():
    row, shard = lax.axis_index("rows"), lax.axis_index("shard")
    return row // 2, row % 2, shard // 2, shard % 2


def first_kernel(sizes, x_hbm, w_hbm, resid_hbm, kept_ref, sent_ref, piece_ref,
                 x, buf, resid, sems, x_sem, resid_sem):
    starts = [sum(sizes[:c]) for c in range(len(sizes))]
    _, _, _, near = place()
    half = x.shape[0] // 2

    def copy(c):
        rows = pl.ds(starts[c], sizes[c])
        return pltpu.make_async_copy(w_hbm.at[rows], buf.at[rows], sems.at[c])

    x_copy = pltpu.make_async_copy(x_hbm, x, x_sem)
    resid_copy = pltpu.make_async_copy(resid_hbm, resid, resid_sem)
    x_copy.start()
    copy(0).start()
    if len(sizes) > 1:
        copy(1).start()
    resid_copy.start()
    x_copy.wait()
    total = None
    for c in range(len(sizes)):
        copy(c).wait()
        if c + 2 < len(sizes):
            copy(c + 2).start()
        rows = pl.ds(starts[c], sizes[c])
        value = jnp.dot(x[:, rows], buf[rows], preferred_element_type=F32)
        total = value if total is None else total + value
        if c == 0:
            resid_copy.wait()
            low, high = resid[:half].astype(F32), resid[half:].astype(F32)
            piece_ref[...] = jnp.where(near == 0, low, high)
    low, high = total[:half], total[half:]
    kept_ref[...] = jnp.where(near == 0, low, high)
    sent_ref[...] = jnp.where(near == 0, high, low).astype(BF)


def first_stage(x, weight, resid):
    inner, width = weight.shape
    group = x.shape[0]
    step = 512 if inner > 512 else inner
    sizes = [min(step, inner - c) for c in range(0, inner, step)]
    args = [pltpu.with_memory_space_constraint(v, pltpu.HBM) for v in (x, weight, resid)]
    half = (group // 2, width)
    return stage(
        partial(first_kernel, sizes), args, [(half, F32), (half, BF), (half, F32)], 5,
        scratch=[
            pltpu.VMEM(x.shape, BF),
            pltpu.VMEM((inner, width), BF),
            pltpu.VMEM(resid.shape, BF),
            pltpu.SemaphoreType.DMA((len(sizes),)),
            pltpu.SemaphoreType.DMA,
            pltpu.SemaphoreType.DMA,
        ],
        limit=inner * width * 2 // MIB + 8, specs=[HBM] * 3,
        flops=2 * group * inner * width, size=2 * inner * width,
    )


def clean_kernel(own_ref, resid_ref, gain_ref, *refs):
    *got, out_ref = refs
    first = own_ref[...]
    for ref in got:
        first = first + ref[...].astype(F32)
    mean_sq = jnp.mean(first * first, axis=1, keepdims=True)
    out_ref[...] = (resid_ref[...] + first * lax.rsqrt(mean_sq + 1e-06) * gain_ref[...]).astype(BF)


def lanes_kernel(blocks, *refs):
    *pieces, out_ref = refs
    lane, _, _, near = place()
    for (k, j), ref in zip([(0, 0)] + blocks, pieces):
        out_ref[lane ^ k, near ^ j] = ref[...]


def split_cores(part, kept_ref, sent_ref, core):
    lanes, group, _ = kept_ref.shape
    for k in range(lanes):
        low = part[2 * k * group : (2 * k + 1) * group]
        high = part[(2 * k + 1) * group : (2 * k + 2) * group]
        kept_ref[k] = jnp.where(core == 0, low, high)
        sent_ref[k] = jnp.where(core == 0, high, low).astype(BF)


def coder_kernel(mine_ref, theirs_ref, shift_ref, enc_ref, bias_ref, dec_ref,
                 latents_ref, hold_ref, kept_ref, sent_ref, centered):
    _, core, _, near = place()
    lanes, group, size = kept_ref.shape
    half = group // 2
    even = core == 0
    for k in range(lanes):
        for j in range(2):
            mine = mine_ref[k, j].astype(F32) - shift_ref[...]
            theirs = theirs_ref[k, j].astype(F32) - shift_ref[...]
            low = 2 * k * group + j * half
            centered[low : low + half] = jnp.where(even, mine, theirs).astype(BF)
            low = low + group
            centered[low : low + half] = jnp.where(even, theirs, mine).astype(BF)
    value = jnp.dot(centered[...], enc_ref[...], preferred_element_type=F32) + bias_ref[...]
    hold_ref[...] = jnp.maximum(value, 0.0).astype(BF)
    latents_ref[...] = hold_ref[...]
    cols = pl.ds(pl.multiple_of((1 - near) * size, 128), size)
    part = jnp.dot(hold_ref[...], dec_ref[:, cols], preferred_element_type=F32)
    split_cores(part, kept_ref, sent_ref, core)


def decode_kernel(hold_ref, dec_ref, kept_ref, sent_ref):
    _, core, _, near = place()
    size = kept_ref.shape[2]
    cols = pl.ds(pl.multiple_of(near * size, 128), size)
    part = jnp.dot(hold_ref[...], dec_ref[:, cols], preferred_element_type=F32)
    split_cores(part, kept_ref, sent_ref, core)


def blocks_kernel(order, kept_ref, got_ref, *refs):
    *outs, hold = refs
    lane, _, _, _ = place()
    hold[...] = kept_ref[...] + got_ref[...].astype(F32)
    for k, ref in zip(order, outs):
        ref[...] = hold[lane ^ k].astype(ref.dtype)


def total_kernel(count, own_ref, *refs):
    got, outs = refs[:count], refs[count:]
    total = own_ref[...]
    for ref in got:
        total = total + ref[...].astype(F32)
    for ref in outs:
        ref[...] = total.astype(ref.dtype)


def recon_kernel(own_ref, bias_ref, *refs):
    *got, out_ref = refs
    _, _, _, near = place()
    half = own_ref.shape[1]
    total = own_ref[...]
    for ref in got:
        total = total + ref[...].astype(F32)
    total = total + jnp.where(near == 0, bias_ref[:, :half], bias_ref[:, half:])
    out_ref[...] = total.astype(BF)


def stream_half(clean_ref, lane, side, recon_ref):
    half = recon_ref.shape[1]
    rows = [clean_ref[lane, j].astype(F32) for j in range(2)]
    clean = jnp.concatenate(rows, axis=0)
    clean = jnp.where(side == 0, clean[:, :half], clean[:, half:])
    return jnp.concatenate([clean, recon_ref[...].astype(F32)], axis=0)


def near_kernel(clean_ref, recon_ref, gain_ref, gate_ref, up_ref, down_ref, gate_out, up_out):
    lane, _, _, near = place()
    half = recon_ref.shape[1]
    rows = pl.ds(pl.multiple_of(near * half, 128), half)
    gain = jnp.where(near == 0, gain_ref[:, :half], gain_ref[:, half:])
    value = (stream_half(clean_ref, lane, near, recon_ref) * gain).astype(BF)
    gate_out[...] = jnp.dot(value, gate_ref[rows], preferred_element_type=F32)
    up_out[...] = jnp.dot(value, up_ref[rows], preferred_element_type=F32)


def far_kernel(fars, early, clean_ref, recon_ref, got_ref, gain_ref, gate_ref, up_ref, down_ref,
               gate_in, up_in, stream_ref, act_ref, *refs):
    lane, _, far, near = place()
    half = recon_ref.shape[1]
    rows = pl.ds(pl.multiple_of((1 - near) * half, 128), half)
    own = stream_half(clean_ref, lane, near, recon_ref)
    other = stream_half(clean_ref, lane, 1 - near, got_ref)
    in_sq = jnp.sum(own * own, axis=1, keepdims=True) + jnp.sum(other * other, axis=1, keepdims=True)
    scale = lax.rsqrt(in_sq / (2 * half) + 1e-06)
    stream_ref[:, :half] = jnp.where(near == 0, own, other)
    stream_ref[:, half:] = jnp.where(near == 0, other, own)
    gain = jnp.where(near == 0, gain_ref[:, half:], gain_ref[:, :half])
    value = (other * gain).astype(BF)
    gate_out = jnp.dot(value, gate_ref[rows], preferred_element_type=F32)
    gate_out = (gate_out + gate_in[...]) * scale
    up_out = jnp.dot(value, up_ref[rows], preferred_element_type=F32)
    up_out = (up_out + up_in[...]) * scale
    act_ref[...] = (jax.nn.gelu(gate_out, approximate=True) * up_out).astype(BF)
    down_pieces(act_ref, down_ref, far, fars[:early], refs)


def down_pieces(act_ref, down_ref, far, offsets, refs):
    size = refs[0].shape[1]
    if size % 128:
        hold = refs[-1]
        second = jnp.dot(act_ref[...], down_ref[...], preferred_element_type=F32)
        for k in range(hold.shape[0]):
            hold[k] = second[:, k * size : (k + 1) * size]
        for k, ref in zip(offsets, refs):
            ref[...] = hold[far ^ k].astype(ref.dtype)
        return
    for k, ref in zip(offsets, refs):
        cols = pl.ds(pl.multiple_of((far ^ k) * size, 128), size)
        value = jnp.dot(act_ref[...], down_ref[:, cols], preferred_element_type=F32)
        ref[...] = value.astype(ref.dtype)


def down_kernel(offsets, act_ref, down_ref, *refs):
    _, _, far, _ = place()
    down_pieces(act_ref, down_ref, far, offsets, refs)


def on_device(
    hidden_in,
    resid,
    down_one,
    gain_one,
    enc_weight,
    enc_bias,
    dec_weight,
    dec_bias,
    gain_pre,
    gate_two,
    up_two,
    down_two,
    gain_post,
):
    n_rows = lax.axis_size("rows")
    n_shard = lax.axis_size("shard")
    group, width = resid.shape
    half = width // 2
    n_lane, n_far = n_rows // 2, n_shard // 2
    core_unit, lane_unit, near_unit, far_unit = n_shard, 2 * n_shard, 1, 2
    plain = list(range(1, n_far))
    first_fars, recon_fars, fars, stat_fars = (
        ([3, 2, 1], [1, 2, 3], [3, 2, 1], [1, 3, 2]) if n_far == 4 else (plain,) * 4
    )
    blocks = [(k, j) for j in (1, 0) for k in reversed(range(n_lane)) if k or j]
    block_units = [k * lane_unit + j * near_unit for k, j in blocks]
    gain_one, dec_bias, gain_pre, enc_bias = (
        v.reshape(1, -1) for v in (gain_one, dec_bias, gain_pre, enc_bias)
    )

    quarter = (group // 2, width)
    kept, sent, resid_part = first_stage(hidden_in, down_one, resid)
    own, sent = stage(
        partial(total_kernel, 1), [kept, swap(sent, near_unit)],
        [(quarter, F32), (quarter, BF)], 12,
    )
    (clean_part,) = stage(
        clean_kernel, [own, resid_part, gain_one] + [swap(sent, k * far_unit) for k in first_fars],
        [(quarter, BF)], 8,
    )

    (mine,) = stage(
        partial(lanes_kernel, blocks),
        [clean_part] + [swap(clean_part, u) for u in block_units],
        [((n_lane, 2) + quarter, BF)], 2,
    )
    theirs = swap(mine, core_unit)

    latent = enc_weight.shape[1]
    rows = n_rows * group
    mine_half = (n_lane, group, half)
    dec = resident(dec_weight)
    latents, hold, kept, sent = stage(
        coder_kernel, [mine, theirs, dec_bias, resident(enc_weight), enc_bias, dec],
        [((rows, latent), BF), ((rows, latent), BF), (mine_half, F32), (mine_half, BF)], 2,
        scratch=[pltpu.VMEM((rows, width), BF)],
        limit=10, flops=3 * rows * latent * width, size=3 * latent * width,
    )
    kept_near, sent_near = stage(
        decode_kernel, [hold, dec], [(mine_half, F32), (mine_half, BF)], 2,
        limit=8, flops=rows * latent * width, size=latent * width,
    )
    part = (group, half)
    outer = list(reversed(range(n_lane)))
    outward = stage(
        partial(blocks_kernel, outer), [kept, swap(sent, core_unit)],
        [(part, BF)] * n_lane, 4, scratch=[pltpu.VMEM(mine_half, F32)],
    )
    own, *inward = stage(
        partial(blocks_kernel, range(n_lane)), [kept_near, swap(sent_near, core_unit)],
        [(part, F32)] + [(part, BF)] * (n_lane - 1), 4, scratch=[pltpu.VMEM(mine_half, F32)],
    )
    got = [swap(v, k * lane_unit + near_unit) for k, v in zip(outer, outward)]
    got += [swap(v, k * lane_unit) for k, v in enumerate(inward, 1)]
    total, sent = stage(partial(total_kernel, len(got)), [own] + got, [(part, F32), (part, BF)], 12)
    (recon_near,) = stage(
        recon_kernel, [total, dec_bias] + [swap(sent, k * far_unit) for k in recon_fars],
        [(part, BF)], 5,
    )
    recon_far = swap(recon_near, near_unit)

    hidden = gate_two.shape[1]
    both = 2 * group
    gate, up, down = resident(gate_two), resident(up_two), resident(down_two)
    gate_part, up_part = stage(
        near_kernel, [mine, recon_near, gain_pre, gate, up, down],
        [((both, hidden), F32)] * 2, 0, limit=10,
        flops=4 * both * hidden * half, size=4 * hidden * half,
    )
    size = width // n_far
    slice_shape = (both, size)
    early = EARLY if size % 128 == 0 else len(fars)
    hold = [] if size % 128 == 0 else [pltpu.VMEM((n_far,) + slice_shape, F32)]
    stream, act, *sent = stage(
        partial(far_kernel, fars, early),
        [mine, recon_near, recon_far, gain_pre, gate, up, down, gate_part, up_part],
        [((both, width), F32), ((both, hidden), BF)] + [(slice_shape, BF)] * early, 0,
        scratch=hold, limit=10, flops=6 * both * hidden * half, size=6 * hidden * half,
    )
    got = [swap(v, k * far_unit) for v, k in zip(sent, fars)]
    *late, own = stage(
        partial(down_kernel, fars[early:] + [0]), [act, down],
        [(slice_shape, BF)] * (len(fars) - early) + [(slice_shape, F32)], 0,
        scratch=hold, limit=8, flops=2 * both * hidden * half, size=2 * hidden * half,
    )
    got += [swap(v, k * far_unit) for v, k in zip(late, fars[early:])]
    (second_bf,) = stage(partial(total_kernel, len(got)), [own] + got, [(slice_shape, BF)], 0)
    second = second_bf.astype(F32) + swap(second_bf, near_unit).astype(F32)
    sq = jnp.sum(second * second, axis=1).reshape(1, -1)
    parts = [sq] + [swap(sq, k * far_unit) for k in reversed(stat_fars)]
    second_sq = sum(parts[1:], parts[0]).reshape(-1, 1)
    index, _ = lax.optimization_barrier((lax.axis_index("shard"), stream))
    columns = width // n_shard
    second_cols = lax.dynamic_slice_in_dim(second, (index % 2) * columns, columns, 1)
    stream_cols = lax.dynamic_slice_in_dim(stream, index * columns, columns, 1)
    post_cols = lax.dynamic_slice_in_dim(gain_post, index * columns, columns, 0)
    outputs = stream_cols + second_cols * lax.rsqrt(second_sq / width + 1e-06) * post_cols
    delta = outputs[group:] - outputs[:group]
    return (latents, delta)


def solution(mesh):
    in_specs = (
        P("rows", "shard"),
        P("rows", None),
        P("shard", None),
        P(),
        P(None, AXES),
        P(AXES),
        P(AXES, None),
        P(),
        P(),
        P(None, "shard"),
        P(None, "shard"),
        P("shard", None),
        P(),
    )
    out_specs = (P(None, AXES), P("rows", "shard"))

    return jax.shard_map(on_device, mesh=mesh, in_specs=in_specs, out_specs=out_specs, check_vma=False)
```

```python
from functools import partial

import jax
import jax.numpy as jnp
from jax import lax
from jax.experimental import pallas as pl
from jax.experimental.pallas import tpu as pltpu
from jax.sharding import PartitionSpec as P


AXES = ("rows", "shard")
BF = jnp.bfloat16
F32 = jnp.float32
MIB = 1 << 20
EARLY = 1
VMEM = pl.BlockSpec(memory_space=pltpu.VMEM)
HBM = pl.BlockSpec(memory_space=pltpu.HBM)


def shape(dims, dtype):
    return jax.ShapeDtypeStruct(tuple(dims), dtype)


def resident(weight):
    return pltpu.with_memory_space_constraint(weight, pltpu.VMEM)


def stage(kernel, args, outs, us, scratch=(), limit=4, specs=None, flops=0, size=0):
    return pl.pallas_call(
        kernel,
        out_shape=[shape(*out) for out in outs],
        in_specs=specs or [VMEM] * len(args),
        out_specs=[VMEM] * len(outs),
        scratch_shapes=list(scratch),
        cost_estimate=pl.CostEstimate(
            flops=flops + int(us * 1.1e9),
            transcendentals=0,
            bytes_accessed=size + int(us * 3e6),
        ),
        compiler_params=pltpu.CompilerParams(vmem_limit_bytes=limit * MIB),
    )(*args)


def swap(value, mask):
    total = lax.axis_size("rows") * lax.axis_size("shard")
    return lax.ppermute(value, AXES, [(i, i ^ mask) for i in range(total)])


def place():
    row, shard = lax.axis_index("rows"), lax.axis_index("shard")
    return row // 2, row % 2, shard // 2, shard % 2


def first_kernel(sizes, x_hbm, w_hbm, resid_hbm, kept_ref, sent_ref, piece_ref,
                 x, buf, resid, sems, x_sem, resid_sem):
    starts = [sum(sizes[:c]) for c in range(len(sizes))]
    _, _, _, near = place()
    half = x.shape[0] // 2

    def copy(c):
        rows = pl.ds(starts[c], sizes[c])
        return pltpu.make_async_copy(w_hbm.at[rows], buf.at[rows], sems.at[c])

    x_copy = pltpu.make_async_copy(x_hbm, x, x_sem)
    resid_copy = pltpu.make_async_copy(resid_hbm, resid, resid_sem)
    x_copy.start()
    copy(0).start()
    if len(sizes) > 1:
        copy(1).start()
    resid_copy.start()
    x_copy.wait()
    total = None
    for c in range(len(sizes)):
        copy(c).wait()
        if c + 2 < len(sizes):
            copy(c + 2).start()
        rows = pl.ds(starts[c], sizes[c])
        value = jnp.dot(x[:, rows], buf[rows], preferred_element_type=F32)
        total = value if total is None else total + value
        if c == 0:
            resid_copy.wait()
            low, high = resid[:half].astype(F32), resid[half:].astype(F32)
            piece_ref[...] = jnp.where(near == 0, low, high)
    low, high = total[:half], total[half:]
    kept_ref[...] = jnp.where(near == 0, low, high)
    sent_ref[...] = jnp.where(near == 0, high, low).astype(BF)


def first_stage(x, weight, resid):
    inner, width = weight.shape
    group = x.shape[0]
    step = 512 if inner > 512 else inner
    sizes = [min(step, inner - c) for c in range(0, inner, step)]
    args = [pltpu.with_memory_space_constraint(v, pltpu.HBM) for v in (x, weight, resid)]
    half = (group // 2, width)
    return stage(
        partial(first_kernel, sizes), args, [(half, F32), (half, BF), (half, F32)], 5,
        scratch=[
            pltpu.VMEM(x.shape, BF),
            pltpu.VMEM((inner, width), BF),
            pltpu.VMEM(resid.shape, BF),
            pltpu.SemaphoreType.DMA((len(sizes),)),
            pltpu.SemaphoreType.DMA,
            pltpu.SemaphoreType.DMA,
        ],
        limit=inner * width * 2 // MIB + 8, specs=[HBM] * 3,
        flops=2 * group * inner * width, size=2 * inner * width,
    )


def clean_kernel(own_ref, resid_ref, gain_ref, *refs):
    *got, out_ref = refs
    first = own_ref[...]
    for ref in got:
        first = first + ref[...].astype(F32)
    mean_sq = jnp.mean(first * first, axis=1, keepdims=True)
    out_ref[...] = (resid_ref[...] + first * lax.rsqrt(mean_sq + 1e-06) * gain_ref[...]).astype(BF)


def lanes_kernel(blocks, *refs):
    *pieces, out_ref = refs
    lane, _, _, near = place()
    for (k, j), ref in zip([(0, 0)] + blocks, pieces):
        out_ref[lane ^ k, near ^ j] = ref[...]


def split_cores(part, kept_ref, sent_ref, core):
    lanes, group, _ = kept_ref.shape
    for k in range(lanes):
        low = part[2 * k * group : (2 * k + 1) * group]
        high = part[(2 * k + 1) * group : (2 * k + 2) * group]
        kept_ref[k] = jnp.where(core == 0, low, high)
        sent_ref[k] = jnp.where(core == 0, high, low).astype(BF)


def coder_kernel(mine_ref, theirs_ref, shift_ref, enc_ref, bias_ref, dec_ref,
                 latents_ref, hold_ref, kept_ref, sent_ref, centered):
    _, core, _, near = place()
    lanes, group, size = kept_ref.shape
    half = group // 2
    even = core == 0
    for k in range(lanes):
        for j in range(2):
            mine = mine_ref[k, j].astype(F32) - shift_ref[...]
            theirs = theirs_ref[k, j].astype(F32) - shift_ref[...]
            low = 2 * k * group + j * half
            centered[low : low + half] = jnp.where(even, mine, theirs).astype(BF)
            low = low + group
            centered[low : low + half] = jnp.where(even, theirs, mine).astype(BF)
    value = jnp.dot(centered[...], enc_ref[...], preferred_element_type=F32) + bias_ref[...]
    hold_ref[...] = jnp.maximum(value, 0.0).astype(BF)
    latents_ref[...] = hold_ref[...]
    cols = pl.ds(pl.multiple_of((1 - near) * size, 128), size)
    part = jnp.dot(hold_ref[...], dec_ref[:, cols], preferred_element_type=F32)
    split_cores(part, kept_ref, sent_ref, core)


def decode_kernel(hold_ref, dec_ref, kept_ref, sent_ref):
    _, core, _, near = place()
    size = kept_ref.shape[2]
    cols = pl.ds(pl.multiple_of(near * size, 128), size)
    part = jnp.dot(hold_ref[...], dec_ref[:, cols], preferred_element_type=F32)
    split_cores(part, kept_ref, sent_ref, core)


def blocks_kernel(order, kept_ref, got_ref, *refs):
    *outs, hold = refs
    lane, _, _, _ = place()
    hold[...] = kept_ref[...] + got_ref[...].astype(F32)
    for k, ref in zip(order, outs):
        ref[...] = hold[lane ^ k].astype(ref.dtype)


def total_kernel(count, own_ref, *refs):
    got, outs = refs[:count], refs[count:]
    total = own_ref[...]
    for ref in got:
        total = total + ref[...].astype(F32)
    for ref in outs:
        ref[...] = total.astype(ref.dtype)


def recon_kernel(own_ref, bias_ref, *refs):
    *got, out_ref = refs
    _, _, _, near = place()
    half = own_ref.shape[1]
    total = own_ref[...]
    for ref in got:
        total = total + ref[...].astype(F32)
    total = total + jnp.where(near == 0, bias_ref[:, :half], bias_ref[:, half:])
    out_ref[...] = total.astype(BF)


def stream_half(clean_ref, lane, side, recon_ref):
    half = recon_ref.shape[1]
    rows = [clean_ref[lane, j].astype(F32) for j in range(2)]
    clean = jnp.concatenate(rows, axis=0)
    clean = jnp.where(side == 0, clean[:, :half], clean[:, half:])
    return jnp.concatenate([clean, recon_ref[...].astype(F32)], axis=0)


def near_kernel(clean_ref, recon_ref, gain_ref, gate_ref, up_ref, down_ref, gate_out, up_out):
    lane, _, _, near = place()
    half = recon_ref.shape[1]
    rows = pl.ds(pl.multiple_of(near * half, 128), half)
    gain = jnp.where(near == 0, gain_ref[:, :half], gain_ref[:, half:])
    value = (stream_half(clean_ref, lane, near, recon_ref) * gain).astype(BF)
    gate_out[...] = jnp.dot(value, gate_ref[rows], preferred_element_type=F32)
    up_out[...] = jnp.dot(value, up_ref[rows], preferred_element_type=F32)


def far_kernel(fars, early, clean_ref, recon_ref, got_ref, gain_ref, gate_ref, up_ref, down_ref,
               gate_in, up_in, stream_ref, act_ref, *refs):
    lane, _, far, near = place()
    half = recon_ref.shape[1]
    rows = pl.ds(pl.multiple_of((1 - near) * half, 128), half)
    own = stream_half(clean_ref, lane, near, recon_ref)
    other = stream_half(clean_ref, lane, 1 - near, got_ref)
    in_sq = jnp.sum(own * own, axis=1, keepdims=True) + jnp.sum(other * other, axis=1, keepdims=True)
    scale = lax.rsqrt(in_sq / (2 * half) + 1e-06)
    stream_ref[:, :half] = jnp.where(near == 0, own, other)
    stream_ref[:, half:] = jnp.where(near == 0, other, own)
    gain = jnp.where(near == 0, gain_ref[:, half:], gain_ref[:, :half])
    value = (other * gain).astype(BF)
    gate_out = jnp.dot(value, gate_ref[rows], preferred_element_type=F32)
    gate_out = (gate_out + gate_in[...]) * scale
    up_out = jnp.dot(value, up_ref[rows], preferred_element_type=F32)
    up_out = (up_out + up_in[...]) * scale
    act_ref[...] = (jax.nn.gelu(gate_out, approximate=True) * up_out).astype(BF)
    down_pieces(act_ref, down_ref, far, fars[:early], refs)


def down_pieces(act_ref, down_ref, far, offsets, refs):
    size = refs[0].shape[1]
    if size % 128:
        hold = refs[-1]
        second = jnp.dot(act_ref[...], down_ref[...], preferred_element_type=F32)
        for k in range(hold.shape[0]):
            hold[k] = second[:, k * size : (k + 1) * size]
        for k, ref in zip(offsets, refs):
            ref[...] = hold[far ^ k].astype(ref.dtype)
        return
    for k, ref in zip(offsets, refs):
        cols = pl.ds(pl.multiple_of((far ^ k) * size, 128), size)
        value = jnp.dot(act_ref[...], down_ref[:, cols], preferred_element_type=F32)
        ref[...] = value.astype(ref.dtype)


def down_kernel(offsets, act_ref, down_ref, *refs):
    _, _, far, _ = place()
    down_pieces(act_ref, down_ref, far, offsets, refs)


def on_device(
    hidden_in,
    resid,
    down_one,
    gain_one,
    enc_weight,
    enc_bias,
    dec_weight,
    dec_bias,
    gain_pre,
    gate_two,
    up_two,
    down_two,
    gain_post,
):
    n_rows = lax.axis_size("rows")
    n_shard = lax.axis_size("shard")
    group, width = resid.shape
    half = width // 2
    n_lane, n_far = n_rows // 2, n_shard // 2
    core_unit, lane_unit, near_unit, far_unit = n_shard, 2 * n_shard, 1, 2
    plain = list(range(1, n_far))
    first_fars, recon_fars, fars, stat_fars = (
        ([3, 2, 1], [1, 2, 3], [3, 2, 1], [1, 3, 2]) if n_far == 4 else (plain,) * 4
    )
    blocks = [(k, j) for j in (1, 0) for k in reversed(range(n_lane)) if k or j]
    block_units = [k * lane_unit + j * near_unit for k, j in blocks]
    gain_one, dec_bias, gain_pre, enc_bias = (
        v.reshape(1, -1) for v in (gain_one, dec_bias, gain_pre, enc_bias)
    )

    quarter = (group // 2, width)
    kept, sent, resid_part = first_stage(hidden_in, down_one, resid)
    own, sent = stage(
        partial(total_kernel, 1), [kept, swap(sent, near_unit)],
        [(quarter, F32), (quarter, BF)], 12,
    )
    (clean_part,) = stage(
        clean_kernel, [own, resid_part, gain_one] + [swap(sent, k * far_unit) for k in first_fars],
        [(quarter, BF)], 8,
    )

    (mine,) = stage(
        partial(lanes_kernel, blocks),
        [clean_part] + [swap(clean_part, u) for u in block_units],
        [((n_lane, 2) + quarter, BF)], 2,
    )
    theirs = swap(mine, core_unit)

    latent = enc_weight.shape[1]
    rows = n_rows * group
    mine_half = (n_lane, group, half)
    dec = resident(dec_weight)
    latents, hold, kept, sent = stage(
        coder_kernel, [mine, theirs, dec_bias, resident(enc_weight), enc_bias, dec],
        [((rows, latent), BF), ((rows, latent), BF), (mine_half, F32), (mine_half, BF)], 2,
        scratch=[pltpu.VMEM((rows, width), BF)],
        limit=10, flops=3 * rows * latent * width, size=3 * latent * width,
    )
    kept_near, sent_near = stage(
        decode_kernel, [hold, dec], [(mine_half, F32), (mine_half, BF)], 2,
        limit=8, flops=rows * latent * width, size=latent * width,
    )
    part = (group, half)
    outer = list(reversed(range(n_lane)))
    outward = stage(
        partial(blocks_kernel, outer), [kept, swap(sent, core_unit)],
        [(part, BF)] * n_lane, 4, scratch=[pltpu.VMEM(mine_half, F32)],
    )
    own, *inward = stage(
        partial(blocks_kernel, range(n_lane)), [kept_near, swap(sent_near, core_unit)],
        [(part, F32)] + [(part, BF)] * (n_lane - 1), 4, scratch=[pltpu.VMEM(mine_half, F32)],
    )
    got = [swap(v, k * lane_unit + near_unit) for k, v in zip(outer, outward)]
    got += [swap(v, k * lane_unit) for k, v in enumerate(inward, 1)]
    total, sent = stage(partial(total_kernel, len(got)), [own] + got, [(part, F32), (part, BF)], 12)
    (recon_near,) = stage(
        recon_kernel, [total, dec_bias] + [swap(sent, k * far_unit) for k in recon_fars],
        [(part, BF)], 5,
    )
    recon_far = swap(recon_near, near_unit)

    hidden = gate_two.shape[1]
    both = 2 * group
    gate, up, down = resident(gate_two), resident(up_two), resident(down_two)
    gate_part, up_part = stage(
        near_kernel, [mine, recon_near, gain_pre, gate, up, down],
        [((both, hidden), F32)] * 2, 0, limit=10,
        flops=4 * both * hidden * half, size=4 * hidden * half,
    )
    size = width // n_far
    slice_shape = (both, size)
    early = EARLY if size % 128 == 0 else len(fars)
    hold = [] if size % 128 == 0 else [pltpu.VMEM((n_far,) + slice_shape, F32)]
    stream, act, *sent = stage(
        partial(far_kernel, fars, early),
        [mine, recon_near, recon_far, gain_pre, gate, up, down, gate_part, up_part],
        [((both, width), F32), ((both, hidden), BF)] + [(slice_shape, BF)] * early, 0,
        scratch=hold, limit=10, flops=6 * both * hidden * half, size=6 * hidden * half,
    )
    got = [swap(v, k * far_unit) for v, k in zip(sent, fars)]
    *late, own = stage(
        partial(down_kernel, fars[early:] + [0]), [act, down],
        [(slice_shape, BF)] * (len(fars) - early) + [(slice_shape, F32)], 0,
        scratch=hold, limit=8, flops=2 * both * hidden * half, size=2 * hidden * half,
    )
    got += [swap(v, k * far_unit) for v, k in zip(late, fars[early:])]
    (second_bf,) = stage(partial(total_kernel, len(got)), [own] + got, [(slice_shape, BF)], 0)
    second = second_bf.astype(F32) + swap(second_bf, near_unit).astype(F32)
    sq = jnp.sum(second * second, axis=1).reshape(1, -1)
    parts = [sq] + [swap(sq, k * far_unit) for k in reversed(stat_fars)]
    second_sq = sum(parts[1:], parts[0]).reshape(-1, 1)
    index, _ = lax.optimization_barrier((lax.axis_index("shard"), stream))
    columns = width // n_shard
    second_cols = lax.dynamic_slice_in_dim(second, (index % 2) * columns, columns, 1)
    stream_cols = lax.dynamic_slice_in_dim(stream, index * columns, columns, 1)
    post_cols = lax.dynamic_slice_in_dim(gain_post, index * columns, columns, 0)
    scale = lax.rsqrt(second_sq / width + 1e-06)
    clean_out, recon_out = (
        stream_cols[rows] + second_cols[rows] * scale[rows] * post_cols
        for rows in (slice(None, group), slice(group, None))
    )
    delta = recon_out - clean_out
    return (latents, delta)


def solution(mesh):
    in_specs = (
        P("rows", "shard"),
        P("rows", None),
        P("shard", None),
        P(),
        P(None, AXES),
        P(AXES),
        P(AXES, None),
        P(),
        P(),
        P(None, "shard"),
        P(None, "shard"),
        P("shard", None),
        P(),
    )
    out_specs = (P(None, AXES), P("rows", "shard"))

    return jax.shard_map(on_device, mesh=mesh, in_specs=in_specs, out_specs=out_specs, check_vma=False)
```
